32 devices in a mesh: row: 1, ang: 32 (over z, y, x, core).
Axes of the slice: x: 2, y: 2, z: 4, core: 2. Of those that a mesh axis runs over, the one named last changes fastest.
Arguments:
- linv_t: bfloat16 [2, 2048, 2048], P(None, 'ang', 'row'), may hold values from -1.5 to 1.5, as said below
- rhs_top: float32 [2, 2048, 16384], P(None, 'row', 'ang'), may hold values from -6 to 6
- factor_t: bfloat16 [2, 2048, 1024], P(None, 'ang', 'row'), may hold values from -0.125 to 0.125
- rhs_rest: float32 [2, 1024, 16384], P(None, 'row', 'ang'), may hold values from -6 to 6
Outputs:
- solved: float32 [2, 2048, 16384], P(None, 'row', 'ang')
- updated: float32 [2, 1024, 16384], P(None, 'row', 'ang')
The draws below stay inside these ranges and needn't reach their ends.
Inputs may be any that keep to these rules, and one draw needn't show every extreme that they name: `linv_t`: lower triangular inverse: entry [c, j, i] is zero where j > i; the diagonal is real and between 0.5 and 1.5.
All inputs are finite; a program needn't handle non-finite values.
Results may differ from the reference program's by a relative error of at most 0.0026.
Values may be sent and summed in bfloat16 or wider, within the bound.
A program may use at most 128 MiB of HBM per device.

```python
import math
import jax
import jax.numpy as jnp
from jax import lax

PANEL = 2048
ANG_DEV = 512
TRAIL = 1024
ANGLES = 16384
N_ANG = 32


def draw_linv_t(key, part):
    first_key, second_key = jax.random.split(jax.random.fold_in(key, 17))
    spread = jax.random.normal(first_key, (2, PANEL, PANEL), jnp.float32)
    spread = spread * (0.7 / math.sqrt(PANEL))
    col_index = lax.broadcasted_iota(jnp.int32, (PANEL, PANEL), 0)
    row_index = lax.broadcasted_iota(jnp.int32, (PANEL, PANEL), 1)
    lower = (col_index < row_index).astype(jnp.float32)
    diag_vals = jax.random.uniform(second_key, (PANEL,), jnp.float32, 0.5, 1.5)
    eye_part = (col_index == row_index).astype(jnp.float32) * diag_vals[None, :]
    real_part = spread[0] * lower + eye_part
    imag_part = spread[1] * lower
    return jnp.stack([real_part, imag_part]).astype(jnp.bfloat16)


def steps_of(key, shape, cuts, least, largest):
    level, own = 1.0, jax.random.fold_in(key, 6)
    for position, shards_of in cuts:
        heights = jnp.exp(jax.random.uniform(jax.random.fold_in(own, position), (shards_of,), jnp.float32, least / len(cuts), largest / len(cuts)))
        level = level * jnp.repeat(heights, shape[position] // shards_of).reshape([-1 if axis == position else 1 for axis in range(len(shape))])
    return level


def normal_values(key, shape, scale, most, cuts=(), held_as=jnp.bfloat16):
    array = jax.random.normal(key, shape, jnp.float32) * scale
    if len(cuts) > 0:
        array = steps_of(key, shape, cuts, -0.22, 0.18) * array
    return jnp.clip(array, min=-most, max=most).astype(held_as)


def setup_inputs(seed: int = 0) -> dict:
    keys = jax.random.split(jax.random.key(seed), 5)
    return {
        "linv_t": draw_linv_t(jax.random.fold_in(keys[4], 71), 0),
        "rhs_top": normal_values(keys[1], (2, PANEL, ANGLES), 1.0, 6.0, ((2, 32),), jnp.float32),
        "factor_t": normal_values(keys[2], (2, PANEL, TRAIL), PANEL ** -0.5, 0.125, ((1, 32),)),
        "rhs_rest": normal_values(keys[3], (2, TRAIL, ANGLES), 1.0, 6.0, ((2, 32),), jnp.float32),
    }


def complex_tdot(left, right, precision):
    dims = (((0,), (0,)), ((), ()))

    def single(first, second):
        return lax.dot_general(first, second, dims, precision=precision, preferred_element_type=jnp.float32)

    real_part = single(left[0], right[0]) - single(left[1], right[1])
    imag_part = single(left[0], right[1]) + single(left[1], right[0])
    return jnp.stack([real_part, imag_part])


def reference(linv_t, rhs_top, factor_t, rhs_rest):
    inverse = linv_t.astype(jnp.float32)
    blocks = N_ANG

    def per_block(index):
        top_block = lax.dynamic_slice_in_dim(rhs_top, index * ANG_DEV, ANG_DEV, 2)
        rest_block = lax.dynamic_slice_in_dim(rhs_rest, index * ANG_DEV, ANG_DEV, 2)
        solved = complex_tdot(inverse, top_block, lax.Precision.HIGHEST)
        update = complex_tdot(factor_t, solved.astype(jnp.bfloat16), None)
        return solved, rest_block - update

    solved_blocks, rest_blocks = lax.map(per_block, jnp.arange(blocks, dtype=jnp.int32))
    solved = jnp.moveaxis(solved_blocks, 0, 2).reshape(2, rhs_top.shape[1], rhs_top.shape[2])
    updated = jnp.moveaxis(rest_blocks, 0, 2).reshape(2, rhs_rest.shape[1], rhs_rest.shape[2])
    return solved, updated
```

```python
import functools

import jax
import jax.numpy as jnp
from jax import lax
from jax.experimental import pallas as pl
from jax.experimental.pallas import tpu as pltpu
from jax.sharding import PartitionSpec as P

BLOCK = 256
KINDS = ((0, 0, "zyx"), (0, 1, "zxy"), (1, 0, "yzx"), (1, 1, "xzy"))
DIMS0 = (((0,), (0,)), ((), ()))


def tdot(first, second):
    return lax.dot_general(first, second, DIMS0, preferred_element_type=jnp.float32)


def split_two(value):
    high = value.astype(jnp.bfloat16)
    low = (value - high.astype(jnp.float32)).astype(jnp.bfloat16)
    return high, low


def general_body(linv_t, rhs_top, factor_t, rhs_rest):
    top_all = lax.all_gather(rhs_top, "row", axis=1, tiled=True)
    high, low = split_two(top_all)
    inverse = lax.all_gather(linv_t, "ang", axis=1, tiled=True)

    def single(first, second):
        return tdot(inverse[first], high[second]) + tdot(inverse[first], low[second])

    solved = jnp.stack([single(0, 0) - single(1, 1), single(0, 1) + single(1, 0)])
    half = lax.all_gather(solved.astype(jnp.bfloat16), "row", axis=1, tiled=True)
    factor = lax.all_gather(factor_t, "ang", axis=1, tiled=True)
    update = jnp.stack(
        [
            tdot(factor[0], half[0]) - tdot(factor[1], half[1]),
            tdot(factor[0], half[1]) + tdot(factor[1], half[0]),
        ]
    )
    return (solved, rhs_rest - update)


def gather_kernel(devices, lin_ref, fac_ref, glin, gfac, recv, send, local):
    levels = devices // 8
    rows = lin_ref.shape[1]
    panel = lin_ref.shape[2]
    classes = panel // BLOCK
    per_class = BLOCK // rows

    me = lax.axis_index("ang")
    core = lax.rem(me, 2)
    x = lax.rem(me // 2, 2)
    y = lax.rem(me // 4, 2)
    z = me // 8
    has_up, has_down = z < levels - 1, z > 0
    targets = (
        me + 2 - 4 * x,
        me + 4 - 8 * y,
        jnp.where(has_up, me + 8, me),
        jnp.where(has_down, me - 8, me),
        me + 1 - 2 * core,
    )

    barrier = pltpu.get_barrier_semaphore()

    def greet(target):
        pl.semaphore_signal(
            barrier, inc=1, device_id={"ang": target}, device_id_type=pl.DeviceIdType.MESH
        )

    for index in (0, 1, 4):
        greet(targets[index])
    pl.when(has_up)(lambda: greet(targets[2]))
    pl.when(has_down)(lambda: greet(targets[3]))
    pl.semaphore_wait(barrier, 3 + has_up.astype(jnp.int32) + has_down.astype(jnp.int32))

    def place(kind, origin, cls):
        which, part, _ = KINDS[kind]
        at_rows = pl.ds(pl.multiple_of(origin * rows, rows), rows)
        if which == 0:
            return glin.at[part, at_rows, pl.ds(cls * BLOCK, panel - cls * BLOCK)]
        return gfac.at[part, at_rows, :]

    def source(kind, cls):
        which, part, _ = KINDS[kind]
        if which == 0:
            return lin_ref.at[part, :, pl.ds(cls * BLOCK, panel - cls * BLOCK)]
        return fac_ref.at[part]

    def by_class(kind, origin, action):
        if KINDS[kind][0] == 0:
            for cls in range(classes):
                pl.when(origin // per_class == cls)(functools.partial(action, cls))
        else:
            action(0)

    def remote(kind, origin, cls, direction, own):
        return pltpu.make_async_remote_copy(
            src_ref=source(kind, cls) if own else place(kind, origin, cls),
            dst_ref=place(kind, origin, cls),
            send_sem=send.at[direction, kind, origin // 2],
            recv_sem=recv.at[kind, origin],
            device_id={"ang": targets[direction]},
            device_id_type=pl.DeviceIdType.MESH,
        )

    def onward(kind, zo, yo, xo):
        same = {"x": x == xo, "y": y == yo, "z": z == zo}
        order = KINDS[kind][2]
        free = {}
        for position, axis in enumerate(order):
            ok = True
            for later in order[position + 1 :]:
                ok = same[later] if ok is True else jnp.logical_and(ok, same[later])
            free[axis] = ok

        def both(first, second):
            return second if first is True else jnp.logical_and(first, second)

        return (
            both(free["x"], same["x"]),
            both(free["y"], same["y"]),
            both(free["z"], jnp.logical_and(z >= zo, has_up)),
            both(free["z"], jnp.logical_and(z <= zo, has_down)),
            True,
        )

    def forward(kind, origin, goes, cls, own, act):
        for direction in range(5):
            copy = remote(kind, origin, cls, direction, own)
            run = copy.start if act == "start" else copy.wait_send
            if goes[direction] is True:
                run()
            else:
                pl.when(goes[direction])(run)

    for kind in range(4):
        goes = onward(kind, z, y, x)
        by_class(kind, me, lambda cls, kind=kind, goes=goes: forward(kind, me, goes, cls, True, "start"))
    copies = (
        pltpu.make_async_copy(lin_ref, glin.at[:, pl.ds(pl.multiple_of(me * rows, rows), rows), :], local.at[0]),
        pltpu.make_async_copy(fac_ref, gfac.at[:, pl.ds(pl.multiple_of(me * rows, rows), rows), :], local.at[1]),
    )
    for copy in copies:
        copy.start()

    chips = devices // 2
    per_level = levels * 4

    def visit(step, carry):
        hops = step // per_level
        chip = lax.rem(step, per_level)
        zo, yo, xo = chip // 4, lax.rem(chip // 2, 2), lax.rem(chip, 2)
        distance = jnp.abs(z - zo) + jnp.abs(y - yo) + jnp.abs(x - xo)
        origin = chip * 2 + core

        @pl.when(distance == hops)
        def _():
            for kind in range(4):
                goes = onward(kind, zo, yo, xo)

                def arrive(cls, kind=kind, goes=goes):
                    remote(kind, origin, cls, 4, False).wait_recv()
                    forward(kind, origin, goes, cls, False, "start")

                by_class(kind, origin, arrive)

        return carry

    lax.fori_loop(per_level, per_level * (levels + 2), visit, 0)

    def finish(chip, carry):
        zo, yo, xo = chip // 4, lax.rem(chip // 2, 2), lax.rem(chip, 2)
        origin = chip * 2 + core
        other = chip * 2 + 1 - core
        for kind in range(4):
            goes = onward(kind, zo, yo, xo)
            by_class(
                kind,
                origin,
                lambda cls, kind=kind, goes=goes: forward(kind, origin, goes, cls, False, "wait"),
            )
            by_class(
                kind,
                other,
                lambda cls, kind=kind: remote(kind, other, cls, 4, False).wait_recv(),
            )
        return carry

    lax.fori_loop(0, chips, finish, 0)
    for copy in copies:
        copy.wait()


def gather(devices, linv_t, factor_t):
    parts, rows, panel = linv_t.shape
    trail = factor_t.shape[2]
    return pl.pallas_call(
        functools.partial(gather_kernel, devices),
        out_shape=(
            jax.ShapeDtypeStruct((parts, rows * devices, panel), linv_t.dtype),
            jax.ShapeDtypeStruct((parts, rows * devices, trail), factor_t.dtype),
        ),
        in_specs=[pl.BlockSpec(memory_space=pl.ANY)] * 2,
        out_specs=[pl.BlockSpec(memory_space=pl.ANY)] * 2,
        scratch_shapes=[
            pltpu.SemaphoreType.DMA((4, devices)),
            pltpu.SemaphoreType.DMA((5, 4, devices // 2)),
            pltpu.SemaphoreType.DMA((2,)),
        ],
        compiler_params=pltpu.CompilerParams(collective_id=0, has_side_effects=True),
    )(linv_t, factor_t)


def solve_kernel(blocks, lin_ref, top_ref, fac_ref, rest_ref, solved_ref, updated_ref, high, low, half, acc):
    step = pl.program_id(0)
    width = top_ref.shape[2]

    @pl.when(step == 0)
    def _():
        @pl.loop(0, blocks)
        def _(index):
            at_rows = pl.ds(pl.multiple_of(index * BLOCK, BLOCK), BLOCK)
            for part in range(2):
                first, second = split_two(top_ref[part, at_rows, :])
                high[at_rows, part * width : (part + 1) * width] = first
                low[at_rows, part * width : (part + 1) * width] = second

    def add(real, imag):
        acc[:, :width] += real[:, :width] - imag[:, width:]
        acc[:, width:] += real[:, width:] + imag[:, :width]

    acc[...] = jnp.zeros_like(acc)

    @pl.when(step < blocks)
    def _():
        @pl.loop(0, step + 1)
        def _(index):
            at_rows = pl.ds(pl.multiple_of(index * BLOCK, BLOCK), BLOCK)
            first, second = high[at_rows, :], low[at_rows, :]
            lreal, limag = lin_ref[0, at_rows, :], lin_ref[1, at_rows, :]
            add(
                tdot(lreal, first) + tdot(lreal, second),
                tdot(limag, first) + tdot(limag, second),
            )

        solved_ref[0] = acc[:, :width]
        solved_ref[1] = acc[:, width:]
        half[pl.ds(pl.multiple_of(step * BLOCK, BLOCK), BLOCK), :] = acc[...].astype(jnp.bfloat16)

    @pl.when(step >= blocks)
    def _():
        @pl.loop(0, blocks)
        def _(index):
            at_rows = pl.ds(pl.multiple_of(index * BLOCK, BLOCK), BLOCK)
            right = half[at_rows, :]
            add(tdot(fac_ref[0, at_rows, :], right), tdot(fac_ref[1, at_rows, :], right))

        updated_ref[0] = rest_ref[0] - acc[:, :width]
        updated_ref[1] = rest_ref[1] - acc[:, width:]


def solve(lin, top, fac, rest):
    parts, panel, width = top.shape
    trail = rest.shape[1]
    blocks, tail = panel // BLOCK, trail // BLOCK
    once = pl.Buffered(1)
    return pl.pallas_call(
        functools.partial(solve_kernel, blocks),
        grid=(blocks + tail,),
        out_shape=(
            jax.ShapeDtypeStruct(top.shape, jnp.float32),
            jax.ShapeDtypeStruct(rest.shape, jnp.float32),
        ),
        in_specs=[
            pl.BlockSpec((parts, panel, BLOCK), lambda i: (0, 0, jnp.minimum(i, blocks - 1))),
            pl.BlockSpec((parts, panel, width), lambda i: (0, 0, 0), pipeline_mode=once),
            pl.BlockSpec((parts, panel, BLOCK), lambda i: (0, 0, jnp.maximum(i - blocks, 0))),
            pl.BlockSpec((parts, BLOCK, width), lambda i: (0, jnp.maximum(i - blocks, 0), 0)),
        ],
        out_specs=[
            pl.BlockSpec((parts, BLOCK, width), lambda i: (0, jnp.minimum(i, blocks - 1), 0)),
            pl.BlockSpec((parts, BLOCK, width), lambda i: (0, jnp.maximum(i - blocks, 0), 0)),
        ],
        scratch_shapes=[
            pltpu.VMEM((panel, 2 * width), jnp.bfloat16),
            pltpu.VMEM((panel, 2 * width), jnp.bfloat16),
            pltpu.VMEM((panel, 2 * width), jnp.bfloat16),
            pltpu.VMEM((BLOCK, 2 * width), jnp.float32),
        ],
        compiler_params=pltpu.CompilerParams(
            dimension_semantics=("arbitrary",), vmem_limit_bytes=58 << 20
        ),
    )(lin, top, fac, rest)


def tree_body(devices, linv_t, rhs_top, factor_t, rhs_rest):
    lin, fac = gather(devices, linv_t, factor_t)
    return solve(lin, rhs_top, fac, rhs_rest)


def solution(mesh):
    devices = mesh.shape["ang"]
    if mesh.shape["row"] == 1 and devices % 8 == 0:
        body = functools.partial(tree_body, devices)
    else:
        body = general_body
    return jax.shard_map(
        body,
        mesh=mesh,
        in_specs=(
            P(None, "ang", "row"),
            P(None, "row", "ang"),
            P(None, "ang", "row"),
            P(None, "row", "ang"),
        ),
        out_specs=(P(None, "row", "ang"), P(None, "row", "ang")),
        check_vma=False,
    )
```

```python
import functools

import jax
import jax.numpy as jnp
from jax import lax
from jax.experimental import pallas as pl
from jax.experimental.pallas import tpu as pltpu
from jax.sharding import PartitionSpec as P

LAG = 2
KINDS = ((0, 0, "zyx"), (0, 1, "zxy"), (1, 0, "yzx"), (1, 1, "xzy"))
DIMS0 = (((0,), (0,)), ((), ()))


def tdot(first, second):
    return lax.dot_general(first, second, DIMS0, preferred_element_type=jnp.float32)


def split_two(value):
    high = value.astype(jnp.bfloat16)
    low = (value - high.astype(jnp.float32)).astype(jnp.bfloat16)
    return high, low


def general_body(linv_t, rhs_top, factor_t, rhs_rest):
    top_all = lax.all_gather(rhs_top, "row", axis=1, tiled=True)
    high, low = split_two(top_all)
    inverse = lax.all_gather(linv_t, "ang", axis=1, tiled=True)

    def single(first, second):
        return tdot(inverse[first], high[second]) + tdot(inverse[first], low[second])

    solved = jnp.stack([single(0, 0) - single(1, 1), single(0, 1) + single(1, 0)])
    half = lax.all_gather(solved.astype(jnp.bfloat16), "row", axis=1, tiled=True)
    factor = lax.all_gather(factor_t, "ang", axis=1, tiled=True)
    update = jnp.stack(
        [
            tdot(factor[0], half[0]) - tdot(factor[1], half[1]),
            tdot(factor[0], half[1]) + tdot(factor[1], half[0]),
        ]
    )
    return (solved, rhs_rest - update)


def fused_kernel(
    devices, lag, lin_ref, top_ref, fac_ref, rest_ref, solved_ref, updated_ref,
    glin, gfac, high, low, acc, upd, recv, send, local,
):
    levels = devices // 8
    chips = devices // 2
    rows = lin_ref.shape[1]
    panel = lin_ref.shape[2]
    width = top_ref.shape[2]
    block = 4 * rows
    blocks = panel // block
    tail = fac_ref.shape[2] // block

    me = lax.axis_index("ang")
    core = lax.rem(me, 2)
    x = lax.rem(me // 2, 2)
    y = lax.rem(me // 4, 2)
    z = me // 8
    has_up, has_down = z < levels - 1, z > 0
    targets = (
        me + 2 - 4 * x,
        me + 4 - 8 * y,
        jnp.where(has_up, me + 8, me),
        jnp.where(has_down, me - 8, me),
        me + 1 - 2 * core,
    )
    mine = pl.ds(pl.multiple_of(me * rows, rows), rows)

    loads = (
        pltpu.make_async_copy(top_ref.at[0], acc.at[:, pl.ds(0, width)], local.at[0]),
        pltpu.make_async_copy(top_ref.at[1], acc.at[:, pl.ds(width, width)], local.at[1]),
        pltpu.make_async_copy(lin_ref, glin.at[:, mine, :], local.at[2]),
        pltpu.make_async_copy(fac_ref, gfac.at[:, mine, :], local.at[3]),
        pltpu.make_async_copy(rest_ref.at[0], upd.at[:, pl.ds(0, width)], local.at[4]),
        pltpu.make_async_copy(rest_ref.at[1], upd.at[:, pl.ds(width, width)], local.at[5]),
    )

    barrier = pltpu.get_barrier_semaphore()

    def greet(target):
        pl.semaphore_signal(
            barrier, inc=1, device_id={"ang": target}, device_id_type=pl.DeviceIdType.MESH
        )

    for index in (0, 1, 4):
        greet(targets[index])
    pl.when(has_up)(lambda: greet(targets[2]))
    pl.when(has_down)(lambda: greet(targets[3]))
    pl.semaphore_wait(barrier, 3 + has_up.astype(jnp.int32) + has_down.astype(jnp.int32))

    def block_at(index):
        return pl.ds(pl.multiple_of(index * block, block), block)

    def place(kind, origin, cls):
        which, part, _ = KINDS[kind]
        at_rows = pl.ds(pl.multiple_of(origin * rows, rows), rows)
        if which == 0:
            return glin.at[part, at_rows, pl.ds(cls * block, panel - cls * block)]
        return gfac.at[part, at_rows, :]

    def source(kind, cls):
        which, part, _ = KINDS[kind]
        if which == 0:
            return lin_ref.at[part, :, pl.ds(cls * block, panel - cls * block)]
        return fac_ref.at[part]

    def by_class(kind, origin, action):
        if KINDS[kind][0] == 0:
            for cls in range(blocks):
                pl.when(origin // 4 == cls)(functools.partial(action, cls))
        else:
            action(0)

    def remote(kind, origin, cls, direction, own):
        return pltpu.make_async_remote_copy(
            src_ref=source(kind, cls) if own else place(kind, origin, cls),
            dst_ref=place(kind, origin, cls),
            send_sem=send.at[direction, kind, origin // 2],
            recv_sem=recv.at[kind, origin],
            device_id={"ang": targets[direction]},
            device_id_type=pl.DeviceIdType.MESH,
        )

    def onward(kind, zo, yo, xo):
        same = {"x": x == xo, "y": y == yo, "z": z == zo}
        order = KINDS[kind][2]
        free = {}
        for position, axis in enumerate(order):
            ok = True
            for later in order[position + 1 :]:
                ok = same[later] if ok is True else jnp.logical_and(ok, same[later])
            free[axis] = ok

        def both(first, second):
            return second if first is True else jnp.logical_and(first, second)

        return (
            both(free["x"], same["x"]),
            both(free["y"], same["y"]),
            both(free["z"], jnp.logical_and(z >= zo, has_up)),
            both(free["z"], jnp.logical_and(z <= zo, has_down)),
            True,
        )

    def forward(kind, origin, goes, cls, own, act):
        for direction in range(5):
            copy = remote(kind, origin, cls, direction, own)
            run = copy.start if act == "start" else copy.wait_send
            if goes[direction] is True:
                run()
            else:
                pl.when(goes[direction])(run)

    def send_own(kind):
        goes = onward(kind, z, y, x)
        by_class(kind, me, lambda cls: forward(kind, me, goes, cls, True, "start"))

    def arrive_other(kind, origin):
        by_class(kind, origin, lambda cls: remote(kind, origin, cls, 4, False).wait_recv())

    send_own(0)
    send_own(1)
    for copy in loads:
        copy.start()
    loads[0].wait()
    loads[1].wait()

    @pl.loop(0, blocks)
    def _(index):
        at_rows = block_at(index)
        for part in range(2):
            cols = slice(part * width, (part + 1) * width)
            first, second = split_two(acc[at_rows, cols])
            high[at_rows, cols] = first
            low[at_rows, cols] = second
        acc[at_rows, :] = jnp.zeros((block, 2 * width), jnp.float32)

    for copy in loads[2:]:
        copy.wait()

    def solve_piece(group, index):
        at_rows, at_cols, to = block_at(group), block_at(index), block_at(index)
        lreal, limag = glin[0, at_rows, at_cols], glin[1, at_rows, at_cols]
        first, second = high[at_rows, :], low[at_rows, :]
        real = tdot(lreal, first) + tdot(lreal, second)
        imag = tdot(limag, first) + tdot(limag, second)
        acc[to, :width] += real[:, :width] - imag[:, width:]
        acc[to, width:] += real[:, width:] + imag[:, :width]

    def update_piece(group, index):
        at_rows, at_cols, to = block_at(group), block_at(index), block_at(index)
        right = high[at_rows, :]
        real = tdot(gfac[0, at_rows, at_cols], right)
        imag = tdot(gfac[1, at_rows, at_cols], right)
        upd[to, :width] += imag[:, width:] - real[:, :width]
        upd[to, width:] -= real[:, width:] + imag[:, :width]

    stores = (
        pltpu.make_async_copy(acc.at[:, pl.ds(0, width)], solved_ref.at[0], local.at[0]),
        pltpu.make_async_copy(acc.at[:, pl.ds(width, width)], solved_ref.at[1], local.at[1]),
        pltpu.make_async_copy(upd.at[:, pl.ds(0, width)], updated_ref.at[0], local.at[2]),
        pltpu.make_async_copy(upd.at[:, pl.ds(width, width)], updated_ref.at[1], local.at[3]),
    )
    solved_at = levels + 3

    def apart(group):
        return jnp.abs(z - group // 2) + jnp.abs(y - lax.rem(group, 2))

    def first_round(group):
        return jnp.maximum(apart(group) + 2 + lag, solved_at)

    def visit(step, carry):
        turn = step // chips
        chip = lax.rem(step, chips)
        zo, yo, xo = chip // 4, lax.rem(chip // 2, 2), lax.rem(chip, 2)
        distance = jnp.abs(z - zo) + jnp.abs(y - yo) + jnp.abs(x - xo)
        origin = chip * 2 + core
        other = chip * 2 + 1 - core

        @pl.when(chip == 0)
        def _():
            @pl.when(turn == lag)
            def _():
                send_own(2)
                send_own(3)

            @pl.when(turn == solved_at)
            def _():
                @pl.loop(0, blocks)
                def _(index):
                    high[block_at(index), :] = acc[block_at(index), :].astype(jnp.bfloat16)

                stores[0].start()
                stores[1].start()

            def arrivals(index, carry):
                group = index // 4

                @pl.when(apart(group) + 2 == turn)
                def _():
                    @pl.when(lax.rem(index, 2) == 1 - core)
                    def _():
                        arrive_other(0, index)
                        arrive_other(1, index)

                @pl.when(first_round(group) == turn)
                def _():
                    @pl.when(lax.rem(index, 2) == 1 - core)
                    def _():
                        arrive_other(2, index)
                        arrive_other(3, index)

                return carry

            lax.fori_loop(0, devices, arrivals, 0)

        for kinds, hops in (((0, 1), turn), ((2, 3), turn - lag)):

            @pl.when(jnp.logical_and(distance == hops, hops > 0))
            def _(kinds=kinds):
                for kind in kinds:
                    goes = onward(kind, zo, yo, xo)

                    def arrive(cls, kind=kind, goes=goes):
                        remote(kind, origin, cls, 4, False).wait_recv()
                        forward(kind, origin, goes, cls, False, "start")

                    by_class(kind, origin, arrive)

        @pl.when(lax.rem(chip, 2) == 0)
        def _():
            index = chip // 2

            @pl.loop(0, blocks)
            def _(group):
                @pl.when(jnp.logical_and(apart(group) + 2 == turn, index >= group))
                def _():
                    solve_piece(group, index)

        every = chips // tail

        @pl.when(lax.rem(chip, every) == 0)
        def _():
            index = chip // every

            @pl.loop(0, blocks)
            def _(group):
                @pl.when(first_round(group) == turn)
                def _():
                    update_piece(group, index)

        return carry

    lax.fori_loop(chips, chips * (levels + 3 + lag), visit, 0)

    stores[2].start()
    stores[3].start()

    def finish(chip, carry):
        zo, yo, xo = chip // 4, lax.rem(chip // 2, 2), lax.rem(chip, 2)
        origin = chip * 2 + core
        for kind in range(4):
            goes = onward(kind, zo, yo, xo)
            by_class(
                kind,
                origin,
                lambda cls, kind=kind, goes=goes: forward(kind, origin, goes, cls, False, "wait"),
            )
        return carry

    lax.fori_loop(0, chips, finish, 0)
    for copy in stores:
        copy.wait()


def fused_body(devices, linv_t, rhs_top, factor_t, rhs_rest):
    parts, rows, panel = linv_t.shape
    trail, width = rhs_rest.shape[1:]
    return pl.pallas_call(
        functools.partial(fused_kernel, devices, LAG),
        out_shape=(
            jax.ShapeDtypeStruct(rhs_top.shape, jnp.float32),
            jax.ShapeDtypeStruct(rhs_rest.shape, jnp.float32),
        ),
        in_specs=[pl.BlockSpec(memory_space=pl.ANY)] * 4,
        out_specs=[pl.BlockSpec(memory_space=pl.ANY)] * 2,
        scratch_shapes=[
            pltpu.VMEM((parts, panel, panel), linv_t.dtype),
            pltpu.VMEM((parts, panel, trail), factor_t.dtype),
            pltpu.VMEM((panel, 2 * width), jnp.bfloat16),
            pltpu.VMEM((panel, 2 * width), jnp.bfloat16),
            pltpu.VMEM((panel, 2 * width), jnp.float32),
            pltpu.VMEM((trail, 2 * width), jnp.float32),
            pltpu.SemaphoreType.DMA((4, devices)),
            pltpu.SemaphoreType.DMA((5, 4, devices // 2)),
            pltpu.SemaphoreType.DMA((6,)),
        ],
        compiler_params=pltpu.CompilerParams(
            collective_id=0, has_side_effects=True, vmem_limit_bytes=60 << 20
        ),
    )(linv_t, rhs_top, factor_t, rhs_rest)


def solution(mesh):
    devices = mesh.shape["ang"]
    if mesh.shape["row"] == 1 and devices % 8 == 0:
        body = functools.partial(fused_body, devices)
    else:
        body = general_body
    return jax.shard_map(
        body,
        mesh=mesh,
        in_specs=(
            P(None, "ang", "row"),
            P(None, "row", "ang"),
            P(None, "ang", "row"),
            P(None, "row", "ang"),
        ),
        out_specs=(P(None, "row", "ang"), P(None, "row", "ang")),
        check_vma=False,
    )
```

```python
import functools

import jax
import jax.numpy as jnp
from jax import lax
from jax.experimental import pallas as pl
from jax.experimental.pallas import tpu as pltpu
from jax.sharding import PartitionSpec as P

LAG = 1
KINDS = ((0, 0, "zyx"), (0, 1, "zxy"), (1, 0, "yzx"), (1, 1, "xzy"))
DIMS0 = (((0,), (0,)), ((), ()))


def tdot(first, second):
    return lax.dot_general(first, second, DIMS0, preferred_element_type=jnp.float32)


def split_two(value):
    high = value.astype(jnp.bfloat16)
    low = (value - high.astype(jnp.float32)).astype(jnp.bfloat16)
    return high, low


def general_body(linv_t, rhs_top, factor_t, rhs_rest):
    top_all = lax.all_gather(rhs_top, "row", axis=1, tiled=True)
    high, low = split_two(top_all)
    inverse = lax.all_gather(linv_t, "ang", axis=1, tiled=True)

    def single(first, second):
        return tdot(inverse[first], high[second]) + tdot(inverse[first], low[second])

    solved = jnp.stack([single(0, 0) - single(1, 1), single(0, 1) + single(1, 0)])
    half = lax.all_gather(solved.astype(jnp.bfloat16), "row", axis=1, tiled=True)
    factor = lax.all_gather(factor_t, "ang", axis=1, tiled=True)
    update = jnp.stack(
        [
            tdot(factor[0], half[0]) - tdot(factor[1], half[1]),
            tdot(factor[0], half[1]) + tdot(factor[1], half[0]),
        ]
    )
    return (solved, rhs_rest - update)


def fused_kernel(
    devices, lag, lin_ref, top_ref, fac_ref, rest_ref, solved_ref, updated_ref,
    glin, gfac, terms, acc, upd, recv, send, local,
):
    levels = devices // 8
    chips = devices // 2
    rows = lin_ref.shape[1]
    panel = lin_ref.shape[2]
    width = top_ref.shape[2]
    block = 4 * rows
    blocks = panel // block
    tail = fac_ref.shape[2] // block

    me = lax.axis_index("ang")
    core = lax.rem(me, 2)
    x = lax.rem(me // 2, 2)
    y = lax.rem(me // 4, 2)
    z = me // 8
    has_up, has_down = z < levels - 1, z > 0
    targets = (
        me + 2 - 4 * x,
        me + 4 - 8 * y,
        jnp.where(has_up, me + 8, me),
        jnp.where(has_down, me - 8, me),
        me + 1 - 2 * core,
    )
    mine = pl.ds(pl.multiple_of(me * rows, rows), rows)

    loads = (
        pltpu.make_async_copy(top_ref, acc, local.at[0]),
        pltpu.make_async_copy(lin_ref, glin.at[:, mine, :], local.at[1]),
        pltpu.make_async_copy(fac_ref, gfac.at[:, mine, :], local.at[2]),
        pltpu.make_async_copy(rest_ref, upd, local.at[3]),
    )

    barrier = pltpu.get_barrier_semaphore()

    def greet(target):
        pl.semaphore_signal(
            barrier, inc=1, device_id={"ang": target}, device_id_type=pl.DeviceIdType.MESH
        )

    for index in (0, 1, 4):
        greet(targets[index])
    pl.when(has_up)(lambda: greet(targets[2]))
    pl.when(has_down)(lambda: greet(targets[3]))
    pl.semaphore_wait(barrier, 3 + has_up.astype(jnp.int32) + has_down.astype(jnp.int32))

    def block_at(index):
        return pl.ds(pl.multiple_of(index * block, block), block)

    def place(kind, origin, cls):
        which, part, _ = KINDS[kind]
        at_rows = pl.ds(pl.multiple_of(origin * rows, rows), rows)
        if which == 0:
            return glin.at[part, at_rows, pl.ds(cls * block, panel - cls * block)]
        return gfac.at[part, at_rows, :]

    def source(kind, cls):
        which, part, _ = KINDS[kind]
        if which == 0:
            return lin_ref.at[part, :, pl.ds(cls * block, panel - cls * block)]
        return fac_ref.at[part]

    def by_class(kind, origin, action):
        if KINDS[kind][0] == 0:
            for cls in range(blocks):
                pl.when(origin // 4 == cls)(functools.partial(action, cls))
        else:
            action(0)

    def remote(kind, origin, cls, direction, own):
        return pltpu.make_async_remote_copy(
            src_ref=source(kind, cls) if own else place(kind, origin, cls),
            dst_ref=place(kind, origin, cls),
            send_sem=send.at[direction, kind, origin // 2],
            recv_sem=recv.at[kind, origin],
            device_id={"ang": targets[direction]},
            device_id_type=pl.DeviceIdType.MESH,
        )

    def onward(kind, zo, yo, xo):
        same = {"x": x == xo, "y": y == yo, "z": z == zo}
        order = KINDS[kind][2]
        free = {}
        for position, axis in enumerate(order):
            ok = True
            for later in order[position + 1 :]:
                ok = same[later] if ok is True else jnp.logical_and(ok, same[later])
            free[axis] = ok

        def both(first, second):
            return second if first is True else jnp.logical_and(first, second)

        return (
            both(free["x"], same["x"]),
            both(free["y"], same["y"]),
            both(free["z"], jnp.logical_and(z >= zo, has_up)),
            both(free["z"], jnp.logical_and(z <= zo, has_down)),
            True,
        )

    def forward(kind, origin, goes, cls, own, act):
        for direction in range(5):
            copy = remote(kind, origin, cls, direction, own)
            run = copy.start if act == "start" else copy.wait_send
            if goes[direction] is True:
                run()
            else:
                pl.when(goes[direction])(run)

    def send_own(kind):
        goes = onward(kind, z, y, x)
        by_class(kind, me, lambda cls: forward(kind, me, goes, cls, True, "start"))

    def arrive_other(kind, origin):
        by_class(kind, origin, lambda cls: remote(kind, origin, cls, 4, False).wait_recv())

    send_own(0)
    send_own(1)
    for copy in loads:
        copy.start()
    loads[0].wait()

    @pl.loop(0, blocks)
    def _(index):
        at_rows = block_at(index)
        for part in range(2):
            first, second = split_two(acc[part, at_rows, :])
            terms[pl.ds(pl.multiple_of((4 * index + 2 * part) * block, block), block), :] = first
            terms[pl.ds(pl.multiple_of((4 * index + 2 * part + 1) * block, block), block), :] = second
            acc[part, at_rows, :] = jnp.zeros((block, width), jnp.float32)

    for copy in loads[1:]:
        copy.wait()

    def solve_piece(group, index):
        at_rows, to = block_at(group), block_at(index)
        lreal, limag = glin[0, at_rows, to].T, glin[1, at_rows, to].T
        right = terms[pl.ds(pl.multiple_of(4 * group * block, block), 4 * block), :]
        real = jnp.concatenate([lreal, lreal, -limag, -limag], axis=1)
        imag = jnp.concatenate([limag, limag, lreal, lreal], axis=1)
        both = jnp.dot(
            jnp.concatenate([real, imag]), right, preferred_element_type=jnp.float32
        )
        acc[0, to, :] += both[:block]
        acc[1, to, :] += both[block:]

    def update_piece(group, index):
        at_rows, to = block_at(group), block_at(index)
        freal, fimag = gfac[0, at_rows, to].T, gfac[1, at_rows, to].T
        right = terms[pl.ds(pl.multiple_of(2 * group * block, block), 2 * block), :]
        real = jnp.concatenate([freal, -fimag], axis=1)
        imag = jnp.concatenate([fimag, freal], axis=1)
        both = jnp.dot(
            jnp.concatenate([real, imag]), right, preferred_element_type=jnp.float32
        )
        upd[0, to, :] -= both[:block]
        upd[1, to, :] -= both[block:]

    def update_block(index):
        to = block_at(index)
        freal, fimag = gfac[0, :, to].T, gfac[1, :, to].T
        lines = []
        for first, second in ((freal, -fimag), (fimag, freal)):
            pieces = []
            for group in range(blocks):
                cols = slice(group * block, (group + 1) * block)
                pieces += [first[:, cols], second[:, cols]]
            lines.append(jnp.concatenate(pieces, axis=1))
        both = jnp.dot(
            jnp.concatenate(lines),
            terms[pl.ds(0, 2 * panel), :],
            preferred_element_type=jnp.float32,
        )
        upd[0, to, :] -= both[:block]
        upd[1, to, :] -= both[block:]

    stores = (
        pltpu.make_async_copy(acc, solved_ref, local.at[0]),
        pltpu.make_async_copy(upd, updated_ref, local.at[1]),
    )
    last_round = levels + 2 + lag
    solved_at = levels + 3

    def apart(group):
        return jnp.abs(z - group // 2) + jnp.abs(y - lax.rem(group, 2))

    def first_round(group):
        return jnp.maximum(apart(group) + 2 + lag, solved_at)

    def solve_count(group, turn):
        return jnp.where(apart(group) + 2 == turn, blocks - group, 0)

    def update_count(group, turn):
        return jnp.where(jnp.logical_and(turn == last_round, group < tail), 1, 0)

    def run_pieces(turn, first, last):
        def find(number, count):
            def scan(group, carry):
                rest, found = carry
                size = count(group, turn)
                found = jnp.where(jnp.logical_and(found < 0, rest < size), group, found)
                return jnp.where(found < 0, rest - size, rest), found

            return lax.fori_loop(0, blocks, scan, (number, jnp.int32(-1)))

        @pl.when(turn < solved_at)
        def _():
            @pl.loop(first, last)
            def _(number):
                rest, group = find(number, solve_count)
                solve_piece(group, group + rest)

        @pl.when(turn >= solved_at)
        def _():
            @pl.loop(first, last)
            def _(number):
                rest, group = find(number, update_count)
                update_block(group)

    def distance_to(chip):
        zo, yo, xo = chip // 4, lax.rem(chip // 2, 2), lax.rem(chip, 2)
        return jnp.abs(z - zo) + jnp.abs(y - yo) + jnp.abs(x - xo)

    def in_round(chip, turn):
        distance = distance_to(chip)
        first = distance == turn
        second = jnp.logical_and(distance == turn - lag, turn > lag)
        return first, second

    def one_round(turn, carry):
        @pl.when(turn == lag)
        def _():
            send_own(2)
            send_own(3)

        @pl.when(turn == solved_at)
        def _():
            @pl.loop(0, blocks)
            def _(index):
                for part in range(2):
                    to = pl.ds(pl.multiple_of((2 * index + part) * block, block), block)
                    terms[to, :] = acc[part, block_at(index), :].astype(jnp.bfloat16)

            stores[0].start()

        def arrivals(chip, carry):
            other = chip * 2 + 1 - core
            group = chip // 2

            @pl.when(apart(group) + 2 == turn)
            def _():
                arrive_other(0, other)
                arrive_other(1, other)

            @pl.when(first_round(group) == turn)
            def _():
                arrive_other(2, other)
                arrive_other(3, other)

            return carry

        lax.fori_loop(0, chips, arrivals, 0)

        def add_pieces(group, total):
            return total + jnp.where(
                turn < solved_at, solve_count(group, turn), update_count(group, turn)
            )

        def add_events(chip, total):
            first, second = in_round(chip, turn)
            return total + jnp.where(jnp.logical_or(first, second), 1, 0)

        pieces = lax.fori_loop(0, blocks, add_pieces, jnp.int32(0))
        slots = lax.fori_loop(0, chips, add_events, jnp.int32(1))

        def visit(chip, slot):
            zo, yo, xo = chip // 4, lax.rem(chip // 2, 2), lax.rem(chip, 2)
            origin = chip * 2 + core
            first, second = in_round(chip, turn)
            either = jnp.logical_or(first, second)

            for kinds, now in (((0, 1), first), ((2, 3), second)):

                @pl.when(now)
                def _(kinds=kinds):
                    for kind in kinds:
                        goes = onward(kind, zo, yo, xo)

                        def arrive(cls, kind=kind, goes=goes):
                            remote(kind, origin, cls, 4, False).wait_recv()
                            forward(kind, origin, goes, cls, False, "start")

                        by_class(kind, origin, arrive)

            @pl.when(either)
            def _():
                run_pieces(turn, slot * pieces // slots, (slot + 1) * pieces // slots)

            return slot + jnp.where(either, 1, 0)

        lax.fori_loop(0, chips, visit, jnp.int32(0))
        run_pieces(turn, (slots - 1) * pieces // slots, pieces)
        return carry

    lax.fori_loop(1, levels + 3 + lag, one_round, 0)

    stores[1].start()

    def finish(chip, carry):
        zo, yo, xo = chip // 4, lax.rem(chip // 2, 2), lax.rem(chip, 2)
        origin = chip * 2 + core
        for kind in range(4):
            goes = onward(kind, zo, yo, xo)
            by_class(
                kind,
                origin,
                lambda cls, kind=kind, goes=goes: forward(kind, origin, goes, cls, False, "wait"),
            )
        return carry

    lax.fori_loop(0, chips, finish, 0)
    for copy in stores:
        copy.wait()


def fused_body(devices, linv_t, rhs_top, factor_t, rhs_rest):
    parts, rows, panel = linv_t.shape
    trail, width = rhs_rest.shape[1:]
    return pl.pallas_call(
        functools.partial(fused_kernel, devices, LAG),
        out_shape=(
            jax.ShapeDtypeStruct(rhs_top.shape, jnp.float32),
            jax.ShapeDtypeStruct(rhs_rest.shape, jnp.float32),
        ),
        in_specs=[pl.BlockSpec(memory_space=pl.ANY)] * 4,
        out_specs=[pl.BlockSpec(memory_space=pl.ANY)] * 2,
        scratch_shapes=[
            pltpu.VMEM((parts, panel, panel), linv_t.dtype),
            pltpu.VMEM((parts, panel, trail), factor_t.dtype),
            pltpu.VMEM((4 * panel, width), jnp.bfloat16),
            pltpu.VMEM(rhs_top.shape, jnp.float32),
            pltpu.VMEM(rhs_rest.shape, jnp.float32),
            pltpu.SemaphoreType.DMA((4, devices)),
            pltpu.SemaphoreType.DMA((5, 4, devices // 2)),
            pltpu.SemaphoreType.DMA((4,)),
        ],
        compiler_params=pltpu.CompilerParams(
            collective_id=0, has_side_effects=True, vmem_limit_bytes=60 << 20
        ),
    )(linv_t, rhs_top, factor_t, rhs_rest)


def solution(mesh):
    devices = mesh.shape["ang"]
    if mesh.shape["row"] == 1 and devices % 8 == 0:
        body = functools.partial(fused_body, devices)
    else:
        body = general_body
    return jax.shard_map(
        body,
        mesh=mesh,
        in_specs=(
            P(None, "ang", "row"),
            P(None, "row", "ang"),
            P(None, "ang", "row"),
            P(None, "row", "ang"),
        ),
        out_specs=(P(None, "row", "ang"), P(None, "row", "ang")),
        check_vma=False,
    )
```
